32 devices in a mesh: members: 2 (over x), row: 16 (over z, y, core).
Axes of the slice: x: 2, y: 2, z: 4, core: 2. Of those that a mesh axis runs over, the one named last changes fastest.
Arguments:
- node_features: bfloat16 [32768, 512], P(('members', 'row')), parts along dimension 0, may hold values from -18 to 18
- nbr_table: int32 [128, 8], P('row'), may hold values from 0 to 27, as said below
- nbr_count: int32 [128], P('row'), may hold values from 4 to 8
- send_block: int32 [256, 1], P('row'), may hold values from 0 to 7
- w_query: bfloat16 [2, 512, 512], replicated, may hold values from -9 to 9
- w_key: bfloat16 [2, 512, 512], replicated, may hold values from -0.7 to 0.7
- w_value: bfloat16 [2, 512, 512], replicated, may hold values from -0.25 to 0.25
- w_out: bfloat16 [2, 512, 512], replicated, may hold values from -0.25 to 0.25
- w_up: bfloat16 [2, 512, 2048], replicated, may hold values from -0.25 to 0.25
- w_down: bfloat16 [2, 2048, 512], replicated, may hold values from -0.125 to 0.125
- w_virtual: bfloat16 [2, 512, 512], replicated, may hold values from -0.25 to 0.25
- gains: float32 [2, 4, 512], replicated, may hold values from 0.25 to 1.75
Outputs:
- latents_out: bfloat16 [32768, 512], P(('members', 'row')), parts along dimension 0
The draws below stay inside these ranges and needn't reach their ends.
There are 2 independent parts, one for each index of `members`. The reference program is written for one: setup_inputs(seed, part) draws one part's arguments, and reference() takes and returns one part's arrays. A program takes and returns all parts, laid end to end along the dimension named above; an argument that names none is the same for every part. Nothing has to cross between parts.
Inputs may be any that keep to these rules, and one draw needn't show every extreme that they name: `nbr_table`: entry t of a row of block g names a block of device g // 8's table: t below 12 are the device's own blocks with 2 blocks of each neighbour along the node order around them, own block b at t = 2 + b; the others are received slots as in the reference program. The first entry of each row is the block itself. Every live entry names a block that exists.
All inputs are finite; a program needn't handle non-finite values.
Results may differ from the reference program's by a relative error of at most 0.007.
Values may be sent and summed in bfloat16 or wider, within the bound.
No kernel may reach another device: no remote copies, remote signals or barrier semaphores. Data moves between devices by JAX's collectives and lax.ppermute only.
A program may use at most 128 MiB of HBM per device.

```python
import math
import jax
import jax.numpy as jnp
from jax import lax

D = 512
FF = 2048
HEADS = 4
BLOCK = 128
NBR = 8
HALO_B = 2
SLOTS = 1
LAYERS = 2
BLK_DEV = 8
NBLK = 128
NODES = 16384
N_ROW = 16


def graph_lists(key):
    devices_count = NBLK // BLK_DEV
    near_count = 2 * HALO_B + BLK_DEV
    counts = jax.random.randint(jax.random.fold_in(key, 11), (NBLK,), NBR // 2, NBR + 1).astype(jnp.int32)
    devices = jnp.arange(devices_count, dtype=jnp.int32)
    ranking = jax.random.randint(jax.random.fold_in(key, 12), (devices_count, devices_count), 0, 1 << 20).astype(jnp.int32)
    ranking = ranking * devices_count + devices[None, :]
    ranking = jnp.where(devices[:, None] == devices[None, :], jnp.int32(1 << 30), ranking)
    order = jnp.argsort(ranking, axis=1, stable=True).astype(jnp.int32)
    most_far = min(devices_count - 1, (NBR // 2 - 1) * BLK_DEV // SLOTS)
    far_live = jax.random.randint(jax.random.fold_in(key, 13), (devices_count,), 1, most_far + 1).astype(jnp.int32)
    per_device = counts.reshape(devices_count, BLK_DEV)
    slot_number = jnp.arange(1, NBR, dtype=jnp.int32)
    live = (slot_number[None, None, :] < per_device[:, :, None]).reshape(devices_count, BLK_DEV * (NBR - 1)).astype(jnp.int32)
    rank = jnp.cumsum(live, axis=1) - 1
    far_position = (live == 1) & (rank < (far_live * SLOTS)[:, None])
    safe_rank = jnp.clip(rank, 0, devices_count * SLOTS - 1)
    peer = jnp.take_along_axis(order, jnp.clip(safe_rank // SLOTS, 0, devices_count - 1), axis=1)
    far_entry = near_count + peer * SLOTS + safe_rank % SLOTS
    lower = jnp.where(devices == 0, HALO_B, 0).astype(jnp.int32)[:, None]
    upper = jnp.where(devices == devices_count - 1, HALO_B + BLK_DEV, near_count).astype(jnp.int32)[:, None]
    random_pick = jax.random.randint(jax.random.fold_in(key, 14), (devices_count, BLK_DEV * (NBR - 1)), 0, 1 << 20).astype(jnp.int32)
    local_entry = lower + random_pick % (upper - lower)
    entries = jnp.where(far_position, far_entry, local_entry).reshape(devices_count, BLK_DEV, NBR - 1)
    own_entry = jnp.broadcast_to((HALO_B + jnp.arange(BLK_DEV, dtype=jnp.int32))[None, :, None], (devices_count, BLK_DEV, 1))
    table = jnp.concatenate((own_entry, entries), axis=2).reshape(NBLK, NBR)
    return (table.astype(jnp.int32), counts)


def draw_nbr_table(key, part):
    return graph_lists(key)[0]


def draw_nbr_count(key, part):
    return graph_lists(key)[1]


def draw_node_features(key, part):
    first, second = jax.random.split(jax.random.fold_in(key, 31), 2)
    position = jnp.arange(NODES, dtype=jnp.float32) / max(NODES - 1, 1)
    offset = jnp.clip(jax.random.normal(second, (D,), jnp.float32), -3.0, 3.0)
    ramp = jnp.exp(jnp.log(3.0) * position)
    base = jnp.clip(jax.random.normal(first, (NODES, D), jnp.float32), -6.0, 6.0)
    values = base + 0.7 * ramp[:, None] * offset[None, :]
    return values.astype(jnp.bfloat16)


def key_weights(key):
    first = jax.random.fold_in(jax.random.fold_in(key, 21), 0)
    drawn = jnp.clip(jax.random.normal(first, (LAYERS, D, D), jnp.float32), -6.0, 6.0) / jnp.sqrt(jnp.float32(D))
    return drawn


def draw_w_key(key, part):
    return key_weights(key).astype(jnp.bfloat16)


def draw_w_query(key, part):
    values = jnp.clip(jax.random.normal(jax.random.fold_in(key, 23), (LAYERS, D, D), jnp.float32), -6.0, 6.0) / jnp.sqrt(jnp.float32(D))
    return values.astype(jnp.bfloat16)


def with_ends(values, rng, low, high):
    shape = values.shape
    place = [jax.random.randint(jax.random.fold_in(rng, axis), (), 0, shape[axis]) for axis in range(len(shape))]
    values = values.at[tuple(place)].set(low)
    longest = shape.index(max(shape))
    place[longest] = (place[longest] + 1) % shape[longest]
    return values.at[tuple(place)].set(high)


def normal_values(rng, shape, deviation, limit, kind=jnp.bfloat16):
    array = deviation * jax.random.normal(rng, shape, jnp.float32)
    return jnp.clip(array, min=-limit, max=limit).astype(kind)


def setup_inputs(seed: int = 0, part: int = 0) -> dict:
    key_of = jax.random.split(jax.random.key(seed), 13)
    part_keys = jax.random.split(jax.random.fold_in(key_of[12], part), 13)
    node_features = draw_node_features(jax.random.fold_in(jax.random.fold_in(key_of[12], part), 71), part)
    nbr_table = draw_nbr_table(jax.random.fold_in(key_of[12], 71), part)
    nbr_count = draw_nbr_count(jax.random.fold_in(key_of[12], 71), part)
    send_block = with_ends(jax.random.randint(key_of[3], (N_ROW * N_ROW, SLOTS), 0, BLK_DEV), jax.random.fold_in(key_of[3], 1), 0, BLK_DEV - 1).astype(jnp.int32)
    w_query = draw_w_query(jax.random.fold_in(key_of[12], 71), part)
    w_key = draw_w_key(jax.random.fold_in(key_of[12], 71), part)
    w_value = normal_values(key_of[6], (LAYERS, D, D), D ** -0.5, 0.25)
    w_out = normal_values(key_of[7], (LAYERS, D, D), D ** -0.5, 0.25)
    w_up = normal_values(key_of[8], (LAYERS, D, FF), D ** -0.5, 0.25)
    w_down = normal_values(key_of[9], (LAYERS, FF, D), FF ** -0.5, 0.125)
    w_virtual = normal_values(key_of[10], (LAYERS, D, D), D ** -0.5, 0.25)
    gains = jnp.clip(1.0 + 0.15 * jax.random.normal(key_of[11], (LAYERS, 4, D), jnp.float32), 0.25, 1.75)
    return {"node_features": node_features, "nbr_table": nbr_table, "nbr_count": nbr_count, "send_block": send_block, "w_query": w_query, "w_key": w_key, "w_value": w_value, "w_out": w_out, "w_up": w_up, "w_down": w_down, "w_virtual": w_virtual, "gains": gains}


def normalize(values, scaling):
    centred = values - lax.optimization_barrier(jnp.mean(values, axis=-1, keepdims=True))
    spread = lax.optimization_barrier(jnp.mean(centred * centred, axis=-1, keepdims=True))
    return centred * lax.rsqrt(spread + 1e-05) * scaling

def attend(queries, table, listed, counts):
    groups, block, width = queries.shape
    slots = listed.shape[1]
    head_size = width // HEADS
    picked = table[listed]
    keys = picked[..., :width].reshape(groups, slots * block, HEADS, head_size)
    values = picked[..., width:].reshape(groups, slots * block, HEADS, head_size)
    heads_q = queries.reshape(groups, block, HEADS, head_size)
    scores = jnp.einsum('gqhd,gkhd->ghqk', heads_q.astype(jnp.float32), keys.astype(jnp.float32)) / math.sqrt(head_size)
    live = (jnp.arange(slots * block, dtype=jnp.int32) // block)[None, :] < counts[:, None]
    scores = jnp.where(live[:, None, None, :], scores, -1e+30)
    top = lax.optimization_barrier(jnp.max(scores, axis=-1, keepdims=True))
    weights = jnp.exp(scores - top)
    probs = (weights / lax.optimization_barrier(jnp.sum(weights, axis=-1, keepdims=True))).astype(jnp.bfloat16)
    context = jnp.einsum('ghqk,gkhd->gqhd', probs.astype(jnp.float32), values.astype(jnp.float32))
    return context.astype(jnp.bfloat16).reshape(groups, block, width)

def reference(node_features, nbr_table, nbr_count, send_block, w_query, w_key, w_value, w_out, w_up, w_down, w_virtual, gains):
    near_count = 2 * HALO_B + BLK_DEV
    owner = (jnp.arange(NBLK, dtype=jnp.int32) // BLK_DEV)[:, None]
    beyond = jnp.maximum(nbr_table - near_count, 0)
    peer = beyond // SLOTS
    sent = send_block[peer * N_ROW + owner, beyond % SLOTS]
    source_blocks = jnp.where(nbr_table < near_count, owner * BLK_DEV + nbr_table - HALO_B, peer * BLK_DEV + sent).astype(jnp.int32)
    latent = node_features
    for layer_index in range(LAYERS):
        current = latent.astype(jnp.float32)
        node_mean = lax.optimization_barrier(jnp.sum(current, axis=0)) / NODES
        normed = normalize(current, gains[layer_index, 0]).astype(jnp.bfloat16)
        queries = jnp.dot(normed, w_query[layer_index], preferred_element_type=jnp.float32).astype(jnp.bfloat16)
        w_pair = jnp.concatenate((w_key[layer_index], w_value[layer_index]), axis=1)
        pairs = jnp.dot(normed, w_pair, preferred_element_type=jnp.float32).astype(jnp.bfloat16).reshape(NBLK, BLOCK, 2 * D)

        def attend_device(operands):
            return attend(operands[0], pairs, operands[1], operands[2])
        context = lax.map(attend_device, (queries.reshape(N_ROW, BLK_DEV, BLOCK, D), source_blocks.reshape(N_ROW, BLK_DEV, NBR), nbr_count.reshape(N_ROW, BLK_DEV)))
        context = context.reshape(NODES, D)
        after_att = current + normalize(jnp.dot(context, w_out[layer_index], preferred_element_type=jnp.float32), gains[layer_index, 1])
        middle = normalize(after_att, gains[layer_index, 2]).astype(jnp.bfloat16)
        hidden = jax.nn.gelu(jnp.dot(middle, w_up[layer_index], preferred_element_type=jnp.float32)).astype(jnp.bfloat16)
        virtual_mean = node_mean.astype(jnp.bfloat16)
        virtual = jnp.dot(virtual_mean[None, :], w_virtual[layer_index], preferred_element_type=jnp.float32)
        output_part = normalize(jnp.dot(hidden, w_down[layer_index], preferred_element_type=jnp.float32), gains[layer_index, 3])
        latent = (after_att + output_part + virtual).astype(jnp.bfloat16)
    return latent
```

```python
import functools
import math

import jax
import jax.numpy as jnp
from jax import lax
from jax.experimental import pallas as pl
from jax.experimental.pallas import tpu as pltpu
from jax.sharding import PartitionSpec as P

HEADS = 4
HALO_B = 2
PAIR = 2
ANY = pl.BlockSpec(memory_space=pl.ANY)
SMEM = pl.BlockSpec(memory_space=pltpu.SMEM)


def normalize(values, scaling):
    centred = values - jnp.mean(values, axis=-1, keepdims=True)
    spread = jnp.mean(centred * centred, axis=-1, keepdims=True)
    return centred * lax.rsqrt(spread + 1e-05) * scaling


def plan_kernel(near, far, table, counts, order, sizes, slots, entries, used, place):
    blocks, listed = table.shape

    def clear(f, c):
        used[f] = 0
        return c

    lax.fori_loop(0, far + 1, clear, 0)

    def scan_block(b, c):
        def scan_entry(j, any_far):
            t = table[b, j]
            is_far = jnp.logical_and(j < counts[b], t >= near)
            used[jnp.where(is_far, t - near, far)] = 1
            return jnp.where(is_far, 1, any_far)

        place[far + b] = lax.fori_loop(0, listed, scan_entry, 0)
        return c

    lax.fori_loop(0, blocks, scan_block, 0)

    def compact(f, n):
        place[f] = n
        slots[n] = f
        return n + used[f]

    n_slots = lax.fori_loop(0, far, compact, 0)

    def take(kind):
        def step(b, n):
            @pl.when(place[far + b] == kind)
            def _():
                order[n] = b

            return n + jnp.where(place[far + b] == kind, 1, 0)

        return step

    n_near = lax.fori_loop(0, blocks, take(0), 0)
    lax.fori_loop(0, blocks, take(1), n_near)
    sizes[0] = n_near
    sizes[1] = n_slots

    def rename_block(b, c):
        def rename(j, c):
            t = table[b, jnp.where(j < counts[b], j, 0)]
            is_far = t >= near
            entries[b, j] = jnp.where(is_far, near + place[jnp.where(is_far, t - near, 0)], t)
            return c

        lax.fori_loop(0, listed, rename, 0)
        return c

    lax.fori_loop(0, blocks, rename_block, 0)


def attend(b, position, entries, counts, q, near_kv, far_kv, context, near):
    block, width = q.shape[1:]
    head = width // HEADS
    listed = entries.shape[1]
    least = listed // 2
    scale = 1.0 / math.sqrt(head)
    count = counts[b]

    def piece(e, lo):
        return near_kv[e, :, lo : lo + head]

    for used in range(least, listed + 1):

        @pl.when(count == used)
        def _():
            for h in range(HEADS):
                lo = h * head
                keys = jnp.concatenate([piece(entries[b, j], lo) for j in range(used)], axis=0)
                values = jnp.concatenate(
                    [piece(entries[b, j], width + lo) for j in range(used)], axis=0
                )
                scores = lax.dot_general(
                    q[b, :, lo : lo + head],
                    keys,
                    (((1,), (1,)), ((), ())),
                    preferred_element_type=jnp.float32,
                )
                top = jnp.max(scores, axis=-1, keepdims=True)
                weights = jnp.exp((scores - top) * scale)
                total = jnp.sum(weights, axis=-1, keepdims=True)
                mixed = jnp.dot(
                    weights.astype(jnp.bfloat16), values, preferred_element_type=jnp.float32
                )
                context[position, :, lo : lo + head] = (mixed / total).astype(jnp.bfloat16)


def finish(rows, latent, context, w_out, w_up, w_down, gains, virtual):
    current = latent.astype(jnp.float32)
    after = current + normalize(
        jnp.dot(context, w_out[...], preferred_element_type=jnp.float32), gains[1:2, :]
    )
    middle = normalize(after, gains[2:3, :]).astype(jnp.bfloat16)
    width = latent.shape[-1]
    total = jnp.zeros((rows, width), jnp.float32)
    for lo in range(0, w_up.shape[1], width):
        hidden = jax.nn.gelu(
            jnp.dot(middle, w_up[:, lo : lo + width], preferred_element_type=jnp.float32)
        ).astype(jnp.bfloat16)
        total += jnp.dot(hidden, w_down[lo : lo + width, :], preferred_element_type=jnp.float32)
    return (after + normalize(total, gains[3:4, :]) + virtual).astype(jnp.bfloat16)


def work_blocks(first, last, order, entries, counts, q, kv, latent, context, weights, gains, virtual,
                next_gain, stage, outs, sems, near):
    w_out, w_up, w_down = weights
    block, width = latent.shape[1:]

    def attention(i, c):
        attend(order[i], i, entries, counts, q, kv, None, context, near)
        return c

    lax.fori_loop(first, last, attention, 0)

    def stores(i):
        b = order[i]
        return [
            pltpu.make_async_copy(stage.at[k, i], outs[k].at[b], sems.at[k, i])
            for k in range(len(outs))
        ]

    def pair(g, c):
        one = first + g * PAIR
        two = jnp.minimum(one + 1, last - 1)
        places = (one, two)
        rows = jnp.concatenate([latent[order[i]] for i in places], axis=0)
        mixed = jnp.concatenate([context[i] for i in places], axis=0)
        result = finish(PAIR * block, rows, mixed, w_out, w_up, w_down, gains, virtual[...])
        stage[0, one] = result[:block]
        stage[0, two] = result[block:]
        if len(outs) > 1:
            normed = normalize(result.astype(jnp.float32), next_gain[0:1, :]).astype(jnp.bfloat16)
            stage[1, one] = normed[:block]
            stage[1, two] = normed[block:]
        for copy in stores(one):
            copy.start()

        @pl.when(one + 1 < last)
        def _():
            for copy in stores(one + 1):
                copy.start()

        return c

    lax.fori_loop(0, (last - first + 1) // PAIR, pair, 0)

    def drain(i, c):
        for copy in stores(i):
            copy.wait()
        return c

    lax.fori_loop(first, last, drain, 0)


def near_kernel(n_out, order, sizes, entries, counts, normed_h, low_h, high_h, latent_h, wq_h, wk_h, wv_h,
                wo_h, wu_h, wd_h, gains_h, next_h, virtual_h, *rest):
    outs = rest[:n_out]
    q_out, kv_out = rest[n_out : n_out + 2]
    (x, latent, wq, wk, wv, wo, wu, wd, gains, nxt, virtual, q, kv, context, stage, in_sems, out_sems,
     kv_sems) = rest[n_out + 2 :]
    blocks, block, width = normed_h.shape
    halo = low_h.shape[0]
    near = blocks + 2 * halo
    sources = [
        (normed_h, x.at[pl.ds(halo, blocks)]),
        (wq_h, wq), (wk_h, wk), (wv_h, wv),
        (low_h, x.at[pl.ds(0, halo)]),
        (high_h, x.at[pl.ds(halo + blocks, halo)]),
        (latent_h, latent), (wo_h, wo), (gains_h, gains), (next_h, nxt), (virtual_h, virtual),
        (wu_h, wu), (wd_h, wd),
    ]
    loads = [pltpu.make_async_copy(s, d, in_sems.at[i]) for i, (s, d) in enumerate(sources)]
    for load in loads:
        load.start()
    for load in loads[:6]:
        load.wait()
    group = 4

    def project_q(g, c):
        at = g * group
        rows = x[pl.ds(halo + at, group)].reshape(group * block, width)
        q[pl.ds(at, group)] = (
            jnp.dot(rows, wq[...], preferred_element_type=jnp.float32)
            .astype(jnp.bfloat16)
            .reshape(group, block, width)
        )
        return c

    lax.fori_loop(0, blocks // group, project_q, 0)

    def project_kv(g, c):
        at = g * group
        rows = x[pl.ds(at, group)].reshape(group * block, width)
        for w, lo in ((wk, 0), (wv, width)):
            kv[pl.ds(at, group), :, lo : lo + width] = (
                jnp.dot(rows, w[...], preferred_element_type=jnp.float32)
                .astype(jnp.bfloat16)
                .reshape(group, block, width)
            )
        return c

    lax.fori_loop(0, near // group, project_kv, 0)
    saves = [
        pltpu.make_async_copy(q, q_out, kv_sems.at[0]),
        pltpu.make_async_copy(kv, kv_out, kv_sems.at[1]),
    ]
    for save in saves:
        save.start()
    for load in loads[6:]:
        load.wait()
    work_blocks(0, sizes[0], order, entries, counts, q, kv, latent, context, (wo, wu, wd), gains, virtual,
                nxt, stage, outs, out_sems, near)
    for save in saves:
        save.wait()


def far_kernel(n_out, order, sizes, slots, entries, counts, far_h, q_h, kv_h, latent_h, wk_h, wv_h, wo_h,
               wu_h, wd_h, gains_h, next_h, virtual_h, *rest):
    outs = rest[n_out : 2 * n_out]
    (x, latent, wk, wv, wo, wu, wd, gains, nxt, virtual, q, kv, context, stage, in_sems, out_sems,
     slot_sems) = rest[2 * n_out :]
    blocks, block, width = q_h.shape
    near = kv_h.shape[0]
    n_slots = sizes[1]
    sources = [
        (wk_h, wk), (wv_h, wv), (q_h, q), (kv_h, kv.at[pl.ds(0, near)]), (latent_h, latent), (wo_h, wo),
        (gains_h, gains), (next_h, nxt), (virtual_h, virtual), (wu_h, wu), (wd_h, wd),
    ]
    loads = [pltpu.make_async_copy(s, d, in_sems.at[i]) for i, (s, d) in enumerate(sources)]

    def fetch(i):
        return pltpu.make_async_copy(far_h.at[slots[i]], x.at[i], slot_sems.at[i])

    def start(i, c):
        fetch(i).start()
        return c

    for load in loads[:2]:
        load.start()
    lax.fori_loop(0, n_slots, start, 0)
    for load in loads[2:]:
        load.start()
    for load in loads[:2]:
        load.wait()

    def land(i, c):
        fetch(i).wait()
        return c

    lax.fori_loop(0, n_slots, land, 0)

    def project(g, c):
        at = g * PAIR
        rows = x[pl.ds(at, PAIR)].reshape(PAIR * block, width)
        for w, lo in ((wk, 0), (wv, width)):
            kv[pl.ds(near + at, PAIR), :, lo : lo + width] = (
                jnp.dot(rows, w[...], preferred_element_type=jnp.float32)
                .astype(jnp.bfloat16)
                .reshape(PAIR, block, width)
            )
        return c

    lax.fori_loop(0, (n_slots + PAIR - 1) // PAIR, project, 0)
    for load in loads[2:]:
        load.wait()
    work_blocks(sizes[0], blocks, order, entries, counts, q, kv, latent, context, (wo, wu, wd), gains,
                virtual, nxt, stage, outs, out_sems, near)


def body(
    node_features,
    nbr_table,
    nbr_count,
    send_block,
    w_query,
    w_key,
    w_value,
    w_out,
    w_up,
    w_down,
    w_virtual,
    gains,
):
    blocks, listed = nbr_table.shape
    rows, width = node_features.shape
    block = rows // blocks
    count = lax.axis_size("row")
    node_total = rows * count
    layers = w_query.shape[0]
    hidden = w_up.shape[2]
    near = blocks + 2 * HALO_B
    far = send_block.size
    bf16, f32, i32 = jnp.bfloat16, jnp.float32, jnp.int32
    shape = jax.ShapeDtypeStruct
    ends = count - 1
    room = far + far % PAIR

    order, sizes, slots, entries = pl.pallas_call(
        functools.partial(plan_kernel, near, far),
        out_shape=[shape((blocks,), i32), shape((2,), i32), shape((far + 1,), i32),
                   shape((blocks, listed), i32)],
        in_specs=[SMEM, SMEM],
        out_specs=[SMEM] * 4,
        scratch_shapes=[pltpu.SMEM((far + 1,), i32), pltpu.SMEM((far + blocks,), i32)],
        name="plan",
    )(nbr_table, nbr_count)

    weight_scratch = [
        pltpu.VMEM((width, width), bf16), pltpu.VMEM((width, width), bf16),
        pltpu.VMEM((width, width), bf16), pltpu.VMEM((width, hidden), bf16),
        pltpu.VMEM((hidden, width), bf16), pltpu.VMEM(gains.shape[1:], f32),
        pltpu.VMEM(gains.shape[1:], f32), pltpu.VMEM((1, width), f32),
    ]
    block_flops = 2 * block * width * (width + 2 * hidden + 2 * listed * block)
    latent = node_features.reshape(blocks, block, width)
    normed = normalize(latent.astype(f32), gains[0, 0]).astype(bf16)
    for layer in range(layers):
        last = layer == layers - 1
        n_out = 1 if last else 2
        received = lax.all_to_all(
            normed[send_block.reshape(-1)], "row", split_axis=0, concat_axis=0, tiled=True
        )
        low = lax.ppermute(normed[blocks - HALO_B :], "row", [(i, i + 1) for i in range(ends)])
        high = lax.ppermute(normed[:HALO_B], "row", [(i + 1, i) for i in range(ends)])
        own_sum = jnp.sum(latent.astype(f32), axis=(0, 1))
        sums = lax.all_to_all(
            jnp.broadcast_to(own_sum[None, None, :], (count, 1, width)), "row", 0, 0, tiled=True
        )
        mean = (jnp.sum(sums, axis=(0, 1)) / node_total).astype(bf16)
        virtual = jnp.dot(mean[None, :], w_virtual[layer], preferred_element_type=f32)
        here = gains[layer]
        following = here if last else gains[layer + 1]
        rows_shape = shape((blocks, block, width), bf16)
        stage_scratch = [
            pltpu.VMEM((blocks, block, width), bf16),
            pltpu.VMEM((n_out, blocks, block, width), bf16),
        ]
        made = pl.pallas_call(
            functools.partial(near_kernel, n_out),
            out_shape=[rows_shape] * n_out + [rows_shape, shape((near, block, 2 * width), bf16)],
            in_specs=[SMEM] * 4 + [ANY] * 13,
            out_specs=[ANY] * (n_out + 2),
            scratch_shapes=[pltpu.VMEM((near, block, width), bf16), pltpu.VMEM((blocks, block, width), bf16),
                            pltpu.VMEM((width, width), bf16)]
            + weight_scratch
            + [pltpu.VMEM((blocks, block, width), bf16), pltpu.VMEM((near, block, 2 * width), bf16)]
            + stage_scratch
            + [pltpu.SemaphoreType.DMA((13,)), pltpu.SemaphoreType.DMA((n_out, blocks)),
               pltpu.SemaphoreType.DMA((2,))],
            cost_estimate=pl.CostEstimate(
                flops=2 * rows * width * width * 4 + blocks * block_flops,
                bytes_accessed=16 << 20, transcendentals=rows * hidden),
            compiler_params=pltpu.CompilerParams(vmem_limit_bytes=48 << 20),
            name="near",
        )(order, sizes, entries, nbr_count, normed, low, high, latent, w_query[layer], w_key[layer],
          w_value[layer], w_out[layer], w_up[layer], w_down[layer], here, following, virtual)
        outs, (q, kv) = made[:n_out], made[n_out:]
        outs = pl.pallas_call(
            functools.partial(far_kernel, n_out),
            out_shape=[rows_shape] * n_out,
            in_specs=[SMEM] * 5 + [ANY] * (12 + n_out),
            out_specs=[ANY] * n_out,
            scratch_shapes=[pltpu.VMEM((room, block, width), bf16), pltpu.VMEM((blocks, block, width), bf16)]
            + weight_scratch
            + [pltpu.VMEM((blocks, block, width), bf16), pltpu.VMEM((near + room, block, 2 * width), bf16)]
            + stage_scratch
            + [pltpu.SemaphoreType.DMA((11,)), pltpu.SemaphoreType.DMA((n_out, blocks)),
               pltpu.SemaphoreType.DMA((room,))],
            input_output_aliases={17 + k: k for k in range(n_out)},
            cost_estimate=pl.CostEstimate(
                flops=4 * far * block * width * width + blocks * block_flops,
                bytes_accessed=16 << 20, transcendentals=rows * hidden),
            compiler_params=pltpu.CompilerParams(vmem_limit_bytes=48 << 20),
            name="far",
        )(order, sizes, slots, entries, nbr_count, received, q, kv, latent, w_key[layer], w_value[layer],
          w_out[layer], w_up[layer], w_down[layer], here, following, virtual, *outs)
        latent = outs[0]
        if not last:
            normed = outs[1]
    return latent.reshape(rows, width)


def solution(mesh):
    in_specs = (
        P(("members", "row"), None),
        P("row", None),
        P("row"),
        P("row", None),
        P(),
        P(),
        P(),
        P(),
        P(),
        P(),
        P(),
        P(),
    )
    out_specs = P(("members", "row"), None)
    return jax.shard_map(body, mesh=mesh, in_specs=in_specs, out_specs=out_specs, check_vma=False)
```

```python
import functools
import math

import jax
import jax.numpy as jnp
from jax import lax
from jax.experimental import pallas as pl
from jax.experimental.pallas import tpu as pltpu
from jax.sharding import PartitionSpec as P

HEADS = 4
HALO_B = 2
PAIR = 2
EXTRA = 8
STRIDE = 2
HBM = pl.BlockSpec(memory_space=pltpu.HBM)
VMEM = pl.BlockSpec(memory_space=pltpu.VMEM)
SMEM = pl.BlockSpec(memory_space=pltpu.SMEM)


def normalize(values, scaling):
    centred = values - jnp.mean(values, axis=-1, keepdims=True)
    spread = jnp.mean(centred * centred, axis=-1, keepdims=True)
    return centred * lax.rsqrt(spread + 1e-05) * scaling


def plan_kernel(near, far, table, counts, order, sizes, entries, used, place):
    blocks, listed = table.shape
    for f in range(far + 1):
        used[f] = 0
    lists_far = []
    for b in range(blocks):
        any_far = 0
        for j in range(listed):
            t = table[b, j]
            is_far = jnp.logical_and(j < counts[b], t >= near)
            used[jnp.where(is_far, t - near, far)] = 1
            any_far = jnp.where(is_far, 1, any_far)
        lists_far.append(any_far)
    n = 0
    for f in range(far):
        place[f] = n
        n = n + used[f]
    sizes[1] = n
    n = 0
    for kind in (0, 1):
        for b in range(blocks):
            match = lists_far[b] == kind
            order[jnp.where(match, n, blocks)] = b
            n = n + jnp.where(match, 1, 0)
        if kind == 0:
            sizes[0] = n
    for b in range(blocks):
        first = table[b, 0]
        for j in range(listed):
            t = jnp.where(j < counts[b], table[b, j], first)
            is_far = t >= near
            entries[b, j] = jnp.where(is_far, near + place[jnp.where(is_far, t - near, 0)], t)


def attend(b, position, entries, counts, q, kv, context):
    block, width = q.shape[1:]
    head = width // HEADS
    listed = entries.shape[1]
    scale = 1.0 / math.sqrt(head)
    count = counts[b]
    sizes = range(listed, 0, -STRIDE)

    for used in sizes:
        least = used - STRIDE if used - STRIDE > 0 else 0

        @pl.when(jnp.logical_and(count > least, count <= used))
        def _():
            for h in range(HEADS):
                lo = h * head
                keys = jnp.concatenate(
                    [kv[entries[b, j], :, lo : lo + head] for j in range(used)], axis=0
                )
                scores = lax.dot_general(
                    q[b, :, lo : lo + head],
                    keys,
                    (((1,), (1,)), ((), ())),
                    preferred_element_type=jnp.float32,
                )
                pieces = [scores[:, j * block : (j + 1) * block] for j in range(used)]
                for j in range(least + 1, used):
                    pieces[j] = pieces[j] + jnp.where(j < count, 0.0, -1e30)
                scores = jnp.concatenate(pieces, axis=1)
                top = jnp.max(scores, axis=-1, keepdims=True)
                weights = jnp.exp((scores - top) * scale)
                total = jnp.sum(weights, axis=-1, keepdims=True)
                values = jnp.concatenate(
                    [kv[entries[b, j], :, width + lo : width + lo + head] for j in range(used)], axis=0
                )
                mixed = jnp.dot(
                    weights.astype(jnp.bfloat16), values, preferred_element_type=jnp.float32
                )
                context[position, :, lo : lo + head] = (mixed / total).astype(jnp.bfloat16)


def finish(layer, latent, context, w_out, w_up, w_down, gains):
    current = latent.astype(jnp.float32)
    after = current + normalize(
        jnp.dot(context, w_out[layer], preferred_element_type=jnp.float32), gains[layer, 1:2, :]
    )
    middle = normalize(after, gains[layer, 2:3, :]).astype(jnp.bfloat16)
    width = latent.shape[-1]
    total = jnp.zeros(latent.shape, jnp.float32)
    for lo in range(0, w_up.shape[2], width):
        hidden = jax.nn.gelu(
            jnp.dot(middle, w_up[layer, :, lo : lo + width], preferred_element_type=jnp.float32)
        ).astype(jnp.bfloat16)
        total += jnp.dot(hidden, w_down[layer, lo : lo + width, :], preferred_element_type=jnp.float32)
    return after + normalize(total, gains[layer, 3:4, :])


def work_blocks(layer, first, last, order, entries, counts, q, kv, latent, context, weights, gains, made):
    block = latent.shape[1]

    def attention(i, c):
        attend(order[i], i, entries, counts, q, kv, context)
        return c

    lax.fori_loop(first, last, attention, 0)

    def pair(g, c):
        one = first + g * PAIR
        two = jnp.minimum(one + 1, last - 1)
        rows = jnp.concatenate([latent[order[one]], latent[order[two]]], axis=0)
        mixed = jnp.concatenate([context[one], context[two]], axis=0)
        result = finish(layer, rows, mixed, *weights, gains)
        made[order[one]] = result[:block]
        made[order[two]] = result[block:]
        return c

    lax.fori_loop(0, (last - first + 1) // PAIR, pair, 0)


def split_sum(total):
    parts = []
    for _ in range(3):
        part = total.astype(jnp.bfloat16)
        parts.append(part.astype(jnp.float32))
        total = total - parts[-1]
    rows = lax.broadcasted_iota(jnp.int32, (EXTRA, total.shape[-1]), 0)
    out = jnp.zeros(rows.shape, jnp.float32)
    for i, part in enumerate(parts):
        out = jnp.where(rows == i, part, out)
    return out.astype(jnp.bfloat16)


def partner(device, step, count):
    if count & (count - 1) == 0:
        return device ^ step
    return (device + step) % count


def origin(device, step, count):
    if count & (count - 1) == 0:
        return device ^ step
    return (device - step) % count


def exchange_steps(count):
    half = count // 2
    if count != 2 * half:
        return list(range(1, count))
    return [half + i // 2 if i % 2 == 0 else i // 2 + 1 for i in range(count - 1)]


def dispatch(me, send_block, normed, extra, sends, tail, head):
    blocks, block, width = normed.shape
    count = len(sends) + 1
    each = send_block.shape[0] // count
    tail[...] = normed[blocks - HALO_B :]
    head[...] = normed[:HALO_B]
    for step, send in zip(exchange_steps(count), sends):
        peer = partner(me[0], step, count)
        for i in range(each):
            send[i * block : (i + 1) * block, :] = normed[send_block[peer * each + i]]
        send[each * block :, :] = extra[...]


def start_kernel(me, send_block, latent_h, gains_h, latent, gains, normed, extra, tail, head, *rest):
    *sends, in_sems = rest
    blocks, block, width = latent.shape
    load_gains = pltpu.make_async_copy(gains_h, gains, in_sems.at[blocks])
    load_gains.start()

    def load(b):
        return pltpu.make_async_copy(latent_h.at[b], latent.at[b], in_sems.at[b])

    for b in range(blocks):
        load(b).start()
    load_gains.wait()

    def step(b, total):
        load(b).wait()
        rows = latent[b].astype(jnp.float32)
        normed[b] = normalize(rows, gains[0, 0:1, :]).astype(jnp.bfloat16)
        return total + jnp.sum(rows, axis=0, keepdims=True)

    extra[...] = split_sum(lax.fori_loop(0, blocks, step, jnp.zeros((1, width), jnp.float32)))
    dispatch(me, send_block, normed, extra, sends, tail, head)


def near_kernel(layer, load, order, sizes, entries, counts, normed, low, high, latent, gains, *rest):
    weights_in, rest = rest[:7], rest[7:]
    q, kv, made, *rest = rest
    if load:
        *weights, context, sems = rest
        loads = [
            pltpu.make_async_copy(weights_in[i], weights[i], sems.at[i]) for i in range(len(weights))
        ]
        for copy in loads:
            copy.start()
    else:
        weights, context = weights_in, rest[0]
    wq, wk, wv, wo, wu, wd, _ = weights
    blocks, block, width = normed.shape
    halo = low.shape[0]
    group = math.gcd(blocks, 4)

    def project(source, at, size, w, out, to, lo):
        rows = source[pl.ds(at, size)].reshape(size * block, width)
        out[pl.ds(to, size), :, lo : lo + width] = (
            jnp.dot(rows, w[layer], preferred_element_type=jnp.float32)
            .astype(jnp.bfloat16)
            .reshape(size, block, width)
        )

    def own(g, c):
        at = g * group
        project(normed, at, group, wq, q, at, 0)
        project(normed, at, group, wk, kv, halo + at, 0)
        project(normed, at, group, wv, kv, halo + at, width)
        return c

    if load:
        for copy in loads[:3]:
            copy.wait()
    lax.fori_loop(0, blocks // group, own, 0)
    for source, to in ((low, 0), (high, halo + blocks)):
        project(source, 0, halo, wk, kv, to, 0)
        project(source, 0, halo, wv, kv, to, width)
    if load:
        for copy in loads[3:]:
            copy.wait()
    work_blocks(layer, 0, sizes[0], order, entries, counts, q, kv, latent, context, (wo, wu, wd), gains, made)


def far_kernel(layer, last, scale, count, me, order, sizes, used, place, entries, counts, send_block, own,
               own_extra, q, kv_in, made_in, latent, gains, wk, wv, wo, wu, wd, w_virtual, *rest):
    received, rest = rest[: count - 1], rest[count - 1 :]
    if last:
        kv, made, following, x, context = rest
    else:
        kv, made, following, normed, extra, tail, head = rest[:7]
        sends = rest[7 : 6 + count]
        x, context = rest[6 + count :]
    blocks, block, width = q.shape
    near = blocks + 2 * HALO_B
    n_slots = sizes[1]
    each = send_block.shape[0] // count

    for step, message in zip([0] + exchange_steps(count), (None,) + tuple(received)):
        peer = origin(me[0], step, count)
        for i in range(each):
            slot = peer * each + i

            @pl.when(used[slot] == 1)
            def _():
                if step:
                    x[place[slot]] = message[i * block : (i + 1) * block, :]
                else:
                    x[place[slot]] = own[send_block[slot]]

    mean = own_extra[...].astype(jnp.float32)
    for message in received:
        mean = mean + message[each * block :, :].astype(jnp.float32)
    mean = jnp.sum(mean, axis=0, keepdims=True) * scale
    mean = jnp.broadcast_to(mean, (EXTRA, width)).astype(jnp.bfloat16)
    virtual = jnp.dot(mean, w_virtual[layer], preferred_element_type=jnp.float32)[0:1]

    def complete(i, total):
        b = order[i]
        rows = (made[b] + virtual).astype(jnp.bfloat16)
        following[b] = rows
        rows = rows.astype(jnp.float32)
        if last:
            return total
        normed[b] = normalize(rows, gains[layer + 1, 0:1, :]).astype(jnp.bfloat16)
        return total + jnp.sum(rows, axis=0, keepdims=True)

    total = lax.fori_loop(0, sizes[0], complete, jnp.zeros((1, width), jnp.float32))
    def project(g, c):
        at = g * PAIR
        rows = x[pl.ds(at, PAIR)].reshape(PAIR * block, width)
        for w, lo in ((wk, 0), (wv, width)):
            kv[pl.ds(near + at, PAIR), :, lo : lo + width] = (
                jnp.dot(rows, w[layer], preferred_element_type=jnp.float32)
                .astype(jnp.bfloat16)
                .reshape(PAIR, block, width)
            )
        return c

    lax.fori_loop(0, (n_slots + PAIR - 1) // PAIR, project, 0)
    work_blocks(layer, sizes[0], blocks, order, entries, counts, q, kv, latent, context, (wo, wu, wd), gains,
                made)
    total = lax.fori_loop(sizes[0], blocks, complete, total)
    if not last:
        extra[...] = split_sum(total)
        dispatch(me, send_block, normed, extra, sends, tail, head)


def body(
    node_features,
    nbr_table,
    nbr_count,
    send_block,
    w_query,
    w_key,
    w_value,
    w_out,
    w_up,
    w_down,
    w_virtual,
    gains,
):
    blocks, listed = nbr_table.shape
    rows, width = node_features.shape
    block = rows // blocks
    count = lax.axis_size("row")
    layers = w_query.shape[0]
    hidden = w_up.shape[2]
    near = blocks + 2 * HALO_B
    far = send_block.size
    bf16, f32, i32 = jnp.bfloat16, jnp.float32, jnp.int32
    shape = jax.ShapeDtypeStruct
    ends = count - 1
    room = far + far % PAIR
    send_block = send_block.reshape(-1)

    def on_chip(value):
        return pltpu.with_memory_space_constraint(value, pltpu.VMEM)

    def off_chip(value):
        return pltpu.with_memory_space_constraint(value, pltpu.HBM)

    def limit(mib):
        return pltpu.CompilerParams(vmem_limit_bytes=mib << 20)

    order, sizes, entries, used, place = pl.pallas_call(
        functools.partial(plan_kernel, near, far),
        out_shape=[shape((blocks + 1,), i32), shape((2,), i32), shape((blocks, listed), i32),
                   shape((far + 1,), i32), shape((far,), i32)],
        in_specs=[SMEM, SMEM],
        out_specs=[SMEM] * 5,
        name="plan",
    )(nbr_table, nbr_count)

    each = far // count
    me = lax.axis_index("row").reshape(1)
    block_flops = 2 * block * width * (width + 2 * hidden + 2 * listed * block)
    extra_vmem = pltpu.VMEM((EXTRA, width), bf16)
    send_shapes = [pltpu.VMEM((HALO_B, block, width), bf16)] * 2 + [
        pltpu.VMEM((each * block + EXTRA, width), bf16)
    ] * (count - 1)
    rows_vmem = pltpu.VMEM((blocks, block, width), bf16)
    latent = node_features.reshape(blocks, block, width)
    latent, scales, normed, extra, tail, head, *sends = pl.pallas_call(
        start_kernel,
        out_shape=[rows_vmem, pltpu.VMEM(gains.shape, f32), rows_vmem, extra_vmem] + send_shapes,
        in_specs=[SMEM, SMEM, HBM, HBM],
        out_specs=[VMEM] * (count + 5),
        scratch_shapes=[pltpu.SemaphoreType.DMA((blocks + 1,))],
        compiler_params=limit(8),
        cost_estimate=pl.CostEstimate(flops=1 << 22, bytes_accessed=4 << 20, transcendentals=rows),
        name="start",
    )(me, send_block, off_chip(latent), off_chip(gains))
    weights = [off_chip(w) for w in (w_query, w_key, w_value, w_out, w_up, w_down, w_virtual)]
    for layer in range(layers):
        last = layer == layers - 1
        low = lax.ppermute(tail, "row", [(i, i + 1) for i in range(ends)])
        high = lax.ppermute(head, "row", [(i + 1, i) for i in range(ends)])
        received = [
            on_chip(lax.ppermute(send, "row", [(i, partner(i, step, count)) for i in range(count)]))
            for step, send in zip(exchange_steps(count), sends)
        ]
        table_vmem = pltpu.VMEM((near + room, block, 2 * width), bf16)
        made_vmem = pltpu.VMEM((blocks, block, width), f32)
        load = layer == 0
        q, kv, made, *held = pl.pallas_call(
            functools.partial(near_kernel, layer, load),
            out_shape=[rows_vmem, table_vmem, made_vmem]
            + ([pltpu.VMEM(w.shape, bf16) for w in weights] if load else []),
            in_specs=[SMEM] * 4 + [VMEM] * 5 + [HBM if load else VMEM] * 7,
            out_specs=[VMEM] * (3 + (7 if load else 0)),
            scratch_shapes=[rows_vmem] + ([pltpu.SemaphoreType.DMA((7,))] if load else []),
            cost_estimate=pl.CostEstimate(
                flops=8 * rows * width * width + blocks * block_flops,
                bytes_accessed=16 << 20, transcendentals=rows * hidden),
            compiler_params=limit(6),
            name="near",
        )(order, sizes, entries, nbr_count, on_chip(normed), on_chip(low), on_chip(high), on_chip(latent),
          on_chip(scales), *(weights if load else map(on_chip, weights)))
        weights = held if load else weights
        outs = pl.pallas_call(
            functools.partial(far_kernel, layer, last, 1.0 / (rows * count), count),
            out_shape=[table_vmem, made_vmem]
            + ([shape((blocks, block, width), bf16)] if last
               else [rows_vmem, rows_vmem, extra_vmem] + send_shapes),
            in_specs=[SMEM] * 8 + [VMEM] * (12 + count),
            out_specs=[VMEM] * (3 if last else 6 + count),
            scratch_shapes=[pltpu.VMEM((room, block, width), bf16), rows_vmem],
            input_output_aliases={11: 0, 12: 1},
            cost_estimate=pl.CostEstimate(
                flops=4 * far * block * width * width + blocks * block_flops,
                bytes_accessed=16 << 20, transcendentals=rows * hidden),
            compiler_params=limit(16),
            name="far",
        )(me, order, sizes, used, place, entries, nbr_count, send_block, on_chip(normed), on_chip(extra),
          on_chip(q), on_chip(kv), on_chip(made), on_chip(latent), on_chip(scales),
          *map(on_chip, weights[1:]), *received)
        latent = outs[2]
        if not last:
            normed, extra, tail, head, *sends = outs[3:]
    return latent.reshape(rows, width)


def solution(mesh):
    in_specs = (
        P(("members", "row"), None),
        P("row", None),
        P("row"),
        P("row", None),
        P(),
        P(),
        P(),
        P(),
        P(),
        P(),
        P(),
        P(),
    )
    out_specs = P(("members", "row"), None)
    return jax.shard_map(body, mesh=mesh, in_specs=in_specs, out_specs=out_specs, check_vma=False)
```

```python
import functools
import math

import jax
import jax.numpy as jnp
from jax import lax
from jax.experimental import pallas as pl
from jax.experimental.pallas import tpu as pltpu
from jax.sharding import PartitionSpec as P

HEADS = 4
HALO_B = 2
PAIR = 2
EXTRA = 8
STRIDE = 2
PART = 1024
HBM = pl.BlockSpec(memory_space=pltpu.HBM)
VMEM = pl.BlockSpec(memory_space=pltpu.VMEM)
SMEM = pl.BlockSpec(memory_space=pltpu.SMEM)


def normalize(values, scaling):
    centred = values - jnp.mean(values, axis=-1, keepdims=True)
    spread = jnp.mean(centred * centred, axis=-1, keepdims=True)
    return centred * lax.rsqrt(spread + 1e-05) * scaling


def plan_kernel(near, far, table, counts, order, sizes, entries, used, place):
    blocks, listed = table.shape
    for f in range(far + 1):
        used[f] = 0
    lists_far = []
    for b in range(blocks):
        any_far = 0
        for j in range(listed):
            t = table[b, j]
            is_far = jnp.logical_and(j < counts[b], t >= near)
            used[jnp.where(is_far, t - near, far)] = 1
            any_far = jnp.where(is_far, 1, any_far)
        lists_far.append(any_far)
    n = 0
    for f in range(far):
        place[f] = n
        n = n + used[f]
    sizes[1] = n
    n = 0
    for kind in (0, 1):
        for b in range(blocks):
            match = lists_far[b] == kind
            order[jnp.where(match, n, blocks)] = b
            n = n + jnp.where(match, 1, 0)
        if kind == 0:
            sizes[0] = n
    for b in range(blocks):
        first = table[b, 0]
        for j in range(listed):
            t = jnp.where(j < counts[b], table[b, j], first)
            is_far = t >= near
            entries[b, j] = jnp.where(is_far, near + place[jnp.where(is_far, t - near, 0)], t)


def attend(b, position, entries, counts, q, kv, context):
    block, width = q.shape[1:]
    head = width // HEADS
    listed = entries.shape[1]
    scale = math.log2(math.e) / math.sqrt(head)
    count = counts[b]
    fewest = listed // 2

    for used in range(listed, fewest - 1, -STRIDE):
        least = used - STRIDE if used > fewest else used - 1

        @pl.when(jnp.logical_and(count > least, count <= used))
        def _():
            rows = [entries[b, j] for j in range(used)]
            scores, tops, weights = [], [], []
            for h in range(HEADS):
                lo = h * head
                keys = jnp.concatenate([kv[e, :, lo : lo + head] for e in rows], axis=0)
                found = lax.dot_general(
                    q[b, :, lo : lo + head],
                    keys,
                    (((1,), (1,)), ((), ())),
                    preferred_element_type=jnp.float32,
                )
                pieces = [found[:, j * block : (j + 1) * block] for j in range(used)]
                for j in range(least + 1, used):
                    pieces[j] = pieces[j] + jnp.where(j < count, 0.0, -1e30)
                scores.append(jnp.concatenate(pieces, axis=1))
                tops.append(jnp.max(scores[h], axis=-1, keepdims=True))
            for h in range(HEADS):
                weights.append(jnp.exp2((scores[h] - tops[h]) * scale))
                lo = width + h * head
                values = jnp.concatenate([kv[e, :, lo : lo + head] for e in rows], axis=0)
                mixed = jnp.dot(
                    weights[h].astype(jnp.bfloat16), values, preferred_element_type=jnp.float32
                )
                total = jnp.sum(weights[h], axis=-1, keepdims=True)
                context[position, :, h * head : (h + 1) * head] = (mixed / total).astype(jnp.bfloat16)


def double_gelu(x):
    inner = math.sqrt(2.0 / math.pi)
    return x + x * jnp.tanh(x * (inner + (inner * 0.044715) * (x * x)))


def finish(layer, latent, context, w_out, w_up, w_down, gains):
    current = latent.astype(jnp.float32)
    after = current + normalize(
        jnp.dot(context, w_out[layer], preferred_element_type=jnp.float32), gains[layer, 1:2, :]
    )
    middle = normalize(after, gains[layer, 2:3, :]).astype(jnp.bfloat16)
    starts = range(0, w_up.shape[2], PART)

    def up(lo):
        return jnp.dot(middle, w_up[layer, :, lo : lo + PART], preferred_element_type=jnp.float32)

    total = jnp.zeros(latent.shape, jnp.float32)
    ahead = up(0)
    for lo in starts:
        now, ahead = ahead, up(lo + PART) if lo + PART < w_up.shape[2] else None
        total += jnp.dot(
            double_gelu(now).astype(jnp.bfloat16), w_down[layer, lo : lo + PART, :],
            preferred_element_type=jnp.float32,
        )
    return after + normalize(total * 0.5, gains[layer, 3:4, :])


def work_blocks(layer, first, last, order, entries, counts, q, kv, latent, context, weights, gains, made):
    block = latent.shape[1]

    def attention(i, c):
        attend(order[i], i, entries, counts, q, kv, context)
        return c

    lax.fori_loop(first, last, attention, 0)

    def pair(g, c):
        one = first + g * PAIR
        two = jnp.minimum(one + 1, last - 1)
        rows = jnp.concatenate([latent[order[one]], latent[order[two]]], axis=0)
        mixed = jnp.concatenate([context[one], context[two]], axis=0)
        result = finish(layer, rows, mixed, *weights, gains)
        made[order[one]] = result[:block]
        made[order[two]] = result[block:]
        return c

    lax.fori_loop(0, (last - first + 1) // PAIR, pair, 0)


def split_sum(total):
    parts = []
    for _ in range(3):
        part = total.astype(jnp.bfloat16)
        parts.append(part.astype(jnp.float32))
        total = total - parts[-1]
    rows = lax.broadcasted_iota(jnp.int32, (EXTRA, total.shape[-1]), 0)
    out = jnp.zeros(rows.shape, jnp.float32)
    for i, part in enumerate(parts):
        out = jnp.where(rows == i, part, out)
    return out.astype(jnp.bfloat16)


def partner(device, step, count):
    if count & (count - 1) == 0:
        return device ^ step
    return (device + step) % count


def origin(device, step, count):
    if count & (count - 1) == 0:
        return device ^ step
    return (device - step) % count


def exchange_steps(count):
    half = count // 2
    if count != 2 * half:
        return list(range(1, count))
    return [half + i // 2 if i % 2 == 0 else i // 2 + 1 for i in range(count - 1)]


def dispatch(me, send_block, normed, extra, sends, tail, head):
    blocks, block, _ = normed.shape
    count = len(sends) + 1
    each = send_block.shape[0] // count
    tail[...] = normed[blocks - HALO_B :]
    head[...] = normed[:HALO_B]
    for step, send in zip(exchange_steps(count), sends):
        peer = partner(me[0], step, count)
        for i in range(each):
            send[i * block : (i + 1) * block, :] = normed[send_block[peer * each + i]]
        send[each * block :, :] = extra[...]


def start_kernel(me, send_block, latent_h, gains_h, latent, gains, normed, extra, tail, head, *rest):
    *sends, in_sems = rest
    blocks, _, width = latent.shape
    load_gains = pltpu.make_async_copy(gains_h, gains, in_sems.at[blocks])
    load_gains.start()

    def load(b):
        return pltpu.make_async_copy(latent_h.at[b], latent.at[b], in_sems.at[b])

    for b in range(blocks):
        load(b).start()
    load_gains.wait()

    def step(b, total):
        load(b).wait()
        rows = latent[b].astype(jnp.float32)
        normed[b] = normalize(rows, gains[0, 0:1, :]).astype(jnp.bfloat16)
        return total + jnp.sum(rows, axis=0, keepdims=True)

    extra[...] = split_sum(lax.fori_loop(0, blocks, step, jnp.zeros((1, width), jnp.float32)))
    dispatch(me, send_block, normed, extra, sends, tail, head)


def near_kernel(layer, load, order, sizes, entries, counts, normed, low, high, latent, gains, *rest):
    weights_in, rest = rest[:7], rest[7:]
    q, kv, made, *rest = rest
    if load:
        *weights, context, sems = rest
        loads = [
            pltpu.make_async_copy(weights_in[i], weights[i], sems.at[i]) for i in range(len(weights))
        ]
        for copy in loads:
            copy.start()
    else:
        weights, context = weights_in, rest[0]
    wq, wk, wv, wo, wu, wd, _ = weights
    blocks, block, width = normed.shape
    halo = low.shape[0]
    group = math.gcd(blocks, 4)

    def project(source, at, size, w, out, to, lo):
        rows = source[pl.ds(at, size)].reshape(size * block, width)
        out[pl.ds(to, size), :, lo : lo + width] = (
            jnp.dot(rows, w[layer], preferred_element_type=jnp.float32)
            .astype(jnp.bfloat16)
            .reshape(size, block, width)
        )

    def own(g, c):
        at = g * group
        project(normed, at, group, wq, q, at, 0)
        project(normed, at, group, wk, kv, halo + at, 0)
        project(normed, at, group, wv, kv, halo + at, width)
        return c

    if load:
        for copy in loads[:3]:
            copy.wait()
    lax.fori_loop(0, blocks // group, own, 0)
    for source, to in ((low, 0), (high, halo + blocks)):
        project(source, 0, halo, wk, kv, to, 0)
        project(source, 0, halo, wv, kv, to, width)
    if load:
        for copy in loads[3:]:
            copy.wait()
    work_blocks(layer, 0, sizes[0], order, entries, counts, q, kv, latent, context, (wo, wu, wd), gains, made)


def far_kernel(layer, last, scale, count, me, order, sizes, used, place, entries, counts, send_block, own,
               own_extra, q, kv_in, made_in, latent, gains, wk, wv, wo, wu, wd, w_virtual, *rest):
    received, rest = rest[: count - 1], rest[count - 1 :]
    if last:
        kv, made, following, x, context = rest
    else:
        kv, made, following, normed, extra, tail, head = rest[:7]
        sends = rest[7 : 6 + count]
        x, context = rest[6 + count :]
    blocks, block, width = q.shape
    near = blocks + 2 * HALO_B
    n_slots = sizes[1]
    each = send_block.shape[0] // count

    for step, message in zip([0] + exchange_steps(count), (None,) + tuple(received)):
        peer = origin(me[0], step, count)
        for i in range(each):
            slot = peer * each + i

            @pl.when(used[slot] == 1)
            def _():
                if step:
                    x[place[slot]] = message[i * block : (i + 1) * block, :]
                else:
                    x[place[slot]] = own[send_block[slot]]

    mean = own_extra[...].astype(jnp.float32)
    for message in received:
        mean = mean + message[each * block :, :].astype(jnp.float32)
    mean = jnp.sum(mean, axis=0, keepdims=True) * scale
    mean = jnp.broadcast_to(mean, (EXTRA, width)).astype(jnp.bfloat16)
    virtual = jnp.dot(mean, w_virtual[layer], preferred_element_type=jnp.float32)[0:1]

    def complete(i, total):
        b = order[i]
        rows = (made[b] + virtual).astype(jnp.bfloat16)
        following[b] = rows
        rows = rows.astype(jnp.float32)
        if last:
            return total
        normed[b] = normalize(rows, gains[layer + 1, 0:1, :]).astype(jnp.bfloat16)
        return total + jnp.sum(rows, axis=0, keepdims=True)

    total = lax.fori_loop(0, sizes[0], complete, jnp.zeros((1, width), jnp.float32))

    def project(g, c):
        at = g * PAIR
        rows = x[pl.ds(at, PAIR)].reshape(PAIR * block, width)
        for w, lo in ((wk, 0), (wv, width)):
            kv[pl.ds(near + at, PAIR), :, lo : lo + width] = (
                jnp.dot(rows, w[layer], preferred_element_type=jnp.float32)
                .astype(jnp.bfloat16)
                .reshape(PAIR, block, width)
            )
        return c

    lax.fori_loop(0, (n_slots + PAIR - 1) // PAIR, project, 0)
    work_blocks(layer, sizes[0], blocks, order, entries, counts, q, kv, latent, context, (wo, wu, wd), gains,
                made)
    total = lax.fori_loop(sizes[0], blocks, complete, total)
    if not last:
        extra[...] = split_sum(total)
        dispatch(me, send_block, normed, extra, sends, tail, head)


def body(
    node_features,
    nbr_table,
    nbr_count,
    send_block,
    w_query,
    w_key,
    w_value,
    w_out,
    w_up,
    w_down,
    w_virtual,
    gains,
):
    blocks, listed = nbr_table.shape
    rows, width = node_features.shape
    block = rows // blocks
    count = lax.axis_size("row")
    layers = w_query.shape[0]
    hidden = w_up.shape[2]
    near = blocks + 2 * HALO_B
    far = send_block.size
    bf16, f32, i32 = jnp.bfloat16, jnp.float32, jnp.int32
    shape = jax.ShapeDtypeStruct
    ends = count - 1
    room = far + far % PAIR
    send_block = send_block.reshape(-1)

    def on_chip(value):
        return pltpu.with_memory_space_constraint(value, pltpu.VMEM)

    def off_chip(value):
        return pltpu.with_memory_space_constraint(value, pltpu.HBM)

    def limit(mib):
        return pltpu.CompilerParams(vmem_limit_bytes=mib << 20)

    order, sizes, entries, used, place = pl.pallas_call(
        functools.partial(plan_kernel, near, far),
        out_shape=[shape((blocks + 1,), i32), shape((2,), i32), shape((blocks, listed), i32),
                   shape((far + 1,), i32), shape((far,), i32)],
        in_specs=[SMEM, SMEM],
        out_specs=[SMEM] * 5,
        name="plan",
    )(nbr_table, nbr_count)

    each = far // count
    me = lax.axis_index("row").reshape(1)
    block_flops = 2 * block * width * (width + 2 * hidden + 2 * listed * block)
    extra_vmem = pltpu.VMEM((EXTRA, width), bf16)
    send_shapes = [pltpu.VMEM((HALO_B, block, width), bf16)] * 2 + [
        pltpu.VMEM((each * block + EXTRA, width), bf16)
    ] * (count - 1)
    rows_vmem = pltpu.VMEM((blocks, block, width), bf16)
    latent = node_features.reshape(blocks, block, width)
    latent, scales, normed, extra, tail, head, *sends = pl.pallas_call(
        start_kernel,
        out_shape=[rows_vmem, pltpu.VMEM(gains.shape, f32), rows_vmem, extra_vmem] + send_shapes,
        in_specs=[SMEM, SMEM, HBM, HBM],
        out_specs=[VMEM] * (count + 5),
        scratch_shapes=[pltpu.SemaphoreType.DMA((blocks + 1,))],
        compiler_params=limit(8),
        cost_estimate=pl.CostEstimate(flops=1 << 22, bytes_accessed=4 << 20, transcendentals=rows),
        name="start",
    )(me, send_block, off_chip(latent), off_chip(gains))
    weights = [off_chip(w) for w in (w_query, w_key, w_value, w_out, w_up, w_down, w_virtual)]
    for layer in range(layers):
        last = layer == layers - 1
        low = lax.ppermute(tail, "row", [(i, i + 1) for i in range(ends)])
        high = lax.ppermute(head, "row", [(i + 1, i) for i in range(ends)])
        received = []
        for step, send in zip(exchange_steps(count), sends):
            pairs = [(i, partner(i, step, count)) for i in range(count)]
            received.append(on_chip(lax.ppermute(send, "row", pairs)))
        table_vmem = pltpu.VMEM((near + room, block, 2 * width), bf16)
        made_vmem = pltpu.VMEM((blocks, block, width), f32)
        load = layer == 0
        q, kv, made, *held = pl.pallas_call(
            functools.partial(near_kernel, layer, load),
            out_shape=[rows_vmem, table_vmem, made_vmem]
            + ([pltpu.VMEM(w.shape, bf16) for w in weights] if load else []),
            in_specs=[SMEM] * 4 + [VMEM] * 5 + [HBM if load else VMEM] * 7,
            out_specs=[VMEM] * (3 + (7 if load else 0)),
            scratch_shapes=[rows_vmem] + ([pltpu.SemaphoreType.DMA((7,))] if load else []),
            cost_estimate=pl.CostEstimate(
                flops=8 * rows * width * width + blocks * block_flops,
                bytes_accessed=16 << 20, transcendentals=rows * hidden),
            compiler_params=limit(6),
            name="near",
        )(order, sizes, entries, nbr_count, on_chip(normed), on_chip(low), on_chip(high), on_chip(latent),
          on_chip(scales), *(weights if load else map(on_chip, weights)))
        weights = held if load else weights
        outs = pl.pallas_call(
            functools.partial(far_kernel, layer, last, 1.0 / (rows * count), count),
            out_shape=[table_vmem, made_vmem]
            + ([shape((blocks, block, width), bf16)] if last
               else [rows_vmem, rows_vmem, extra_vmem] + send_shapes),
            in_specs=[SMEM] * 8 + [VMEM] * (12 + count),
            out_specs=[VMEM] * (3 if last else 6 + count),
            scratch_shapes=[pltpu.VMEM((room, block, width), bf16), rows_vmem],
            input_output_aliases={11: 0, 12: 1},
            cost_estimate=pl.CostEstimate(
                flops=4 * far * block * width * width + blocks * block_flops,
                bytes_accessed=16 << 20, transcendentals=rows * hidden),
            compiler_params=limit(16),
            name="far",
        )(me, order, sizes, used, place, entries, nbr_count, send_block, on_chip(normed), on_chip(extra),
          on_chip(q), on_chip(kv), on_chip(made), on_chip(latent), on_chip(scales),
          *map(on_chip, weights[1:]), *received)
        latent = outs[2]
        if not last:
            normed, extra, tail, head, *sends = outs[3:]
    return latent.reshape(rows, width)


def solution(mesh):
    in_specs = (
        P(("members", "row"), None),
        P("row", None),
        P("row"),
        P("row", None),
        P(),
        P(),
        P(),
        P(),
        P(),
        P(),
        P(),
        P(),
    )
    out_specs = P(("members", "row"), None)
    return jax.shard_map(body, mesh=mesh, in_specs=in_specs, out_specs=out_specs, check_vma=False)
```
